32 devices in a mesh: sec: 4 (over x, core), sub: 8 (over z, y).
Axes of the slice: x: 2, y: 2, z: 4, core: 2. Of those that a mesh axis runs over, the one named last changes fastest.
Arguments:
- schur: bfloat16 [8, 1024, 1024], P('sub', 'sec'), may hold values from -0.1875 to 0.1875
- neumann: bfloat16 [8, 1024, 1024], P('sub', 'sec'), may hold values from -0.1875 to 0.1875
- constraint_weights: bfloat16 [8, 1024, 128], P('sub', 'sec'), may hold values from -0.1875 to 0.1875
- coarse_inverse: bfloat16 [8, 768, 768], P('sub', 'sec'), may hold values from -0.21875 to 0.21875
- solution: bfloat16 [8, 1024, 128], P('sub', 'sec'), may hold values from -6 to 6
- load: bfloat16 [8, 1024, 128], P('sub', 'sec'), may hold values from -6 to 6
- neighbours: int32 [8, 4], P('sub'), may hold values from 0 to 7, as said below
- face_index: int32 [8, 1024], P('sub', 'sec'), may hold values from 0 to 255, as said below
- coarse_dof: int32 [8, 128], P('sub'), may hold values from 0 to 6143, as said below
Outputs:
- precond: bfloat16 [8, 1024, 128], P('sub', 'sec')
- image: bfloat16 [8, 1024, 128], P('sub', 'sec')
The draws below stay inside these ranges and needn't reach their ends.
Inputs may be any that keep to these rules, and one draw needn't show every extreme that they name: `neighbours`: the subdomain glued to face f of subdomain i is another subdomain whose column c // 1 is the column i // 1 of i or the one before or after it, cyclically over 8 columns. `face_index`: for each subdomain and face, the entries of the face's 256 unknowns are a permutation of 0 to 255. `coarse_dof`: constraint k of subdomain i maps to an unknown of the cluster of column i // 1 or of the column before or after it, cyclically. Each cluster has 64 coarse unknowns that are used, and each used unknown is the unknown of exactly two constraints.
All inputs are finite; a program needn't handle non-finite values.
Results may differ from the reference program's by a relative error of at most 0.0058.
Values may be sent and summed in bfloat16 or wider, within the bound.
No kernel may reach another device: no remote copies, remote signals or barrier semaphores. Data moves between devices by JAX's collectives and lax.ppermute only.
A program may use at most 64 MiB of HBM per device.

```python
import jax
import jax.numpy as jnp
from jax import lax

ORDER = 1024
FACES = 4
FACE_LEN = 256
CONS = 128
CDOF = 768
COLS = 128
MB = 1
SD_DEV = 1
SUBDOMAINS = 8
CLUSTERS = 8
COLS_ALL = 128


def draw_neighbours(key, part):
    key_one, key_two = jax.random.split(jax.random.fold_in(key, 11))
    column_count = SUBDOMAINS // SD_DEV
    home_col = (jnp.arange(SUBDOMAINS) // SD_DEV)[:, None]
    slot_own = (jnp.arange(SUBDOMAINS) % SD_DEV)[:, None]
    offset = jax.random.randint(key_one, (SUBDOMAINS, FACES), -1, 2)
    slot_pick = jax.random.randint(key_two, (SUBDOMAINS, FACES), 0, SD_DEV)
    clash = (offset == 0) & (slot_pick == slot_own)
    slot_pick = jnp.where(clash, (slot_pick + 1) % SD_DEV, slot_pick)
    clash = (offset == 0) & (slot_pick == slot_own)
    offset = jnp.where(clash, 1, offset)
    offset = offset.at[0, 0].set(-1).at[SD_DEV, 0].set(-1)
    slot_pick = slot_pick.at[0, 0].set(SD_DEV - 1).at[SD_DEV, 0].set(0)
    return ((home_col + offset) % column_count * SD_DEV + slot_pick).astype(jnp.int32)


def draw_face_index(key, part):
    sub_keys = jax.random.split(jax.random.fold_in(key, 23), SUBDOMAINS * FACES)
    perms = jax.vmap(lambda sub_key: jax.random.permutation(sub_key, FACE_LEN))(sub_keys)
    return perms.reshape(SUBDOMAINS, ORDER).astype(jnp.int32)


def draw_coarse_dof(key, part):
    key_one, key_two = jax.random.split(jax.random.fold_in(key, 37))
    column_count = SUBDOMAINS // SD_DEV
    per_column = SD_DEV * CONS
    used_count = per_column // 2
    half_used = used_count // 2
    inner_keys = jax.random.split(key_one, column_count)
    inner = jax.vmap(lambda sub_key: jax.random.permutation(sub_key, CDOF - 2))(inner_keys).astype(jnp.int32) + 1
    first_slot = jnp.zeros((column_count, 1), jnp.int32)
    last_slot = jnp.full((column_count, 1), CDOF - 1, jnp.int32)
    used_slots = jnp.concatenate([first_slot, last_slot, inner[:, :used_count - 2]], axis=1)
    role_keys = jax.random.split(key_two, column_count)
    roles = jax.vmap(lambda sub_key: jax.random.permutation(sub_key, per_column))(role_keys).astype(jnp.int32)
    columns = jnp.arange(column_count, dtype=jnp.int32)[:, None]
    is_own = roles < used_count
    is_next = (roles >= used_count) & (roles < used_count + half_used)
    target = jnp.where(is_own, columns, jnp.where(is_next, (columns + 1) % column_count, (columns - 1 + column_count) % column_count))
    position = jnp.where(is_own, roles, roles - used_count)
    chosen = used_slots[target, position]
    return (target * CDOF + chosen).reshape(SUBDOMAINS, CONS).astype(jnp.int32)


def shard_levels(stream_key, extent, pieces, least, high):
    def one(dim, shards_of):
        steps = jax.random.uniform(jax.random.fold_in(jax.random.fold_in(stream_key, 6), dim), (shards_of,), jnp.float32, least / len(pieces), high / len(pieces))
        return jnp.repeat(jnp.exp(steps), extent[dim] // shards_of).reshape((-1,) + (1,) * (len(extent) - dim - 1))

    factor_of = one(*pieces[0])
    for cut in pieces[1:]:
        factor_of = factor_of * one(*cut)
    return factor_of


def bell_draw(own_key, extent, scale, limit, cuts=(), held_as=jnp.bfloat16):
    level = shard_levels(own_key, extent, cuts, -0.22, 0.18) if cuts else 1.0
    values = jax.random.normal(own_key, extent, jnp.float32) * scale * level
    return jnp.minimum(jnp.maximum(values, -limit), limit).astype(held_as)


def setup_inputs(seed: int = 0) -> dict:
    arg_keys = jax.random.split(jax.random.key(seed), 10)
    return {
        "schur": bell_draw(arg_keys[0], (SUBDOMAINS, ORDER, ORDER), ORDER ** -0.5, 0.1875, ((0, 8), (1, 4))),
        "neumann": bell_draw(arg_keys[1], (SUBDOMAINS, ORDER, ORDER), ORDER ** -0.5, 0.1875, ((0, 8), (1, 4))),
        "constraint_weights": bell_draw(arg_keys[2], (SUBDOMAINS, ORDER, CONS), ORDER ** -0.5, 0.1875, ((0, 8), (1, 4))),
        "coarse_inverse": bell_draw(arg_keys[3], (CLUSTERS, CDOF, CDOF), CDOF ** -0.5, 0.21875, ((0, 8), (1, 4))),
        "solution": bell_draw(arg_keys[4], (SUBDOMAINS, ORDER, COLS_ALL), 1.0, 6.0, ((0, 8), (1, 4))),
        "load": bell_draw(arg_keys[5], (SUBDOMAINS, ORDER, COLS_ALL), 1.0, 6.0, ((0, 8), (1, 4))),
        "neighbours": draw_neighbours(jax.random.fold_in(arg_keys[9], 71), 0),
        "face_index": draw_face_index(jax.random.fold_in(arg_keys[9], 71), 0),
        "coarse_dof": draw_coarse_dof(jax.random.fold_in(arg_keys[9], 71), 0),
    }


def apply_blocks(blocks, field):
    def single(pair):
        return jnp.dot(pair[0].astype(jnp.float32), pair[1].astype(jnp.float32), precision=lax.Precision.HIGHEST)
    return lax.map(single, (blocks, field))


def join_faces(field, neighbours, face_index):
    face_len = ORDER // FACES
    face_of = (jnp.arange(ORDER) // face_len).astype(jnp.int32)
    nbr_rows = neighbours[:, face_of]
    src_rows = face_of[None, :] * face_len + face_index
    return field + field[nbr_rows, src_rows]


def reference(schur, neumann, constraint_weights, coarse_inverse, solution, load, neighbours, face_index, coarse_dof):
    flat_dof = coarse_dof.reshape(-1)
    weights_t = jnp.swapaxes(constraint_weights, 1, 2)
    precond_parts = []
    image_parts = []
    for micro_batch in range(MB):
        first_col = micro_batch * COLS
        iterate = solution[:, :, first_col:first_col + COLS]
        residual = load[:, :, first_col:first_col + COLS].astype(jnp.float32) - apply_blocks(schur, iterate)
        assembled = join_faces(residual, neighbours, face_index).astype(jnp.bfloat16)
        constraint_values = apply_blocks(weights_t, assembled)
        coarse_rhs = jax.ops.segment_sum(constraint_values.reshape(-1, COLS), flat_dof, num_segments=CLUSTERS * CDOF)
        coarse_solution = apply_blocks(coarse_inverse, coarse_rhs.astype(jnp.bfloat16).reshape(CLUSTERS, CDOF, COLS)).astype(jnp.bfloat16)
        picked = jnp.take(coarse_solution.reshape(-1, COLS), flat_dof, axis=0).reshape(SUBDOMAINS, CONS, COLS)
        correction = apply_blocks(neumann, assembled) + apply_blocks(constraint_weights, picked)
        precond = (0.5 * join_faces(correction, neighbours, face_index)).astype(jnp.bfloat16)
        image = apply_blocks(schur, precond).astype(jnp.bfloat16)
        precond_parts.append(precond)
        image_parts.append(image)
    return jnp.concatenate(precond_parts, axis=2), jnp.concatenate(image_parts, axis=2)
```

```python
import jax
import jax.numpy as jnp
from jax import lax
from jax.sharding import PartitionSpec as P

F32 = jnp.float32
BF16 = jnp.bfloat16
KINDS = ("A2", "B2", "A3", "B3")


def partner(kind, i, count):
    forward = {
        "A": i % 2 == 0,
        "B": i % 2 == 1,
        "A2": i % 4 < 2,
        "B2": i % 4 >= 2,
        "A3": i % 2 == 0,
        "B3": i % 2 == 1,
    }[kind]
    step = {"2": 2, "3": 3}.get(kind[-1], 1)
    return (i + step if forward else i - step) % count


def swap_columns(array, kind):
    count = lax.axis_size("sub")
    return lax.ppermute(array, "sub", [(i, partner(kind, i, count)) for i in range(count)])


def swap_by_section(array, kinds):
    sections, count = lax.axis_size("sec"), lax.axis_size("sub")
    moves = [
        (s * count + i, s * count + partner(kinds[s % len(kinds)], i, count))
        for s in range(sections)
        for i in range(count)
    ]
    return lax.ppermute(array, ("sec", "sub"), moves)


def swap_cores(array):
    return lax.ppermute(array, "sec", [(i, i ^ 1) for i in range(lax.axis_size("sec"))])


def dot(a, b):
    return jnp.dot(a, b, preferred_element_type=F32)


def encode_dof(dof, column, count, coarse_len):
    near = (dof // coarse_len - column + 1) % count
    slot = dof % coarse_len
    parts = -(-coarse_len // 128)
    rows = jnp.stack([near * parts + slot // 128, slot % 128]).astype(BF16)
    return jnp.pad(rows, ((0, 14), (0, 0)))


def decode_dof(rows, offset, coarse_len):
    parts = -(-coarse_len // 128)
    whole = rows[:2].astype(F32).astype(jnp.int32)
    cluster = offset + 1 + whole[0] // parts
    return cluster, whole[0] % parts * 128 + whole[1]


def local(
    schur,
    neumann,
    constraint_weights,
    coarse_inverse,
    solution,
    load,
    neighbours,
    face_index,
    coarse_dof,
):
    s_rows, n_rows, weights = schur[0], neumann[0], constraint_weights[0]
    c_rows = coarse_inverse[0]
    face_len, cons = weights.shape
    coarse_part, coarse_len = c_rows.shape
    used = cons // 2
    column, section = lax.axis_index("sub"), lax.axis_index("sec")
    count = lax.axis_size("sub")
    core = section % 2

    even = column % 2 == 0
    off1 = jnp.where(even, 1, -1)
    off2 = jnp.where(column % 4 < 2, 2, -2)
    off3 = jnp.where(even, 3, -3)

    own_code = encode_dof(coarse_dof[0], column, count, coarse_len)
    far_code = swap_by_section(own_code, KINDS)
    first = jnp.concatenate([weights, own_code])
    near_b = swap_columns(first, "B")
    near_a = swap_columns(first, "A")

    iterate = lax.all_gather(solution[0], "sec", axis=0, tiled=True)
    residual = load[0].astype(F32) - dot(s_rows, iterate)

    residual_half = residual.astype(BF16)
    res_b = swap_columns(residual_half, "B")
    res_a = swap_columns(residual_half, "A")

    nbr = neighbours[0, section]
    want_a = ((nbr - column - off1) % count) == 0
    positions = lax.broadcasted_iota(jnp.int32, (face_len, face_len), 1)
    selector = (face_index[0][:, None] == positions).astype(BF16)

    dec = lambda rows, off: decode_dof(rows, off, coarse_len)
    parts3 = [
        dec(own_code, 0),
        dec(near_a[face_len:], off1),
        dec(near_b[face_len:], -off1),
    ]
    clus3 = jnp.concatenate([p[0] for p in parts3])
    slot3 = jnp.concatenate([p[1] for p in parts3])
    key3 = jnp.where(clus3 == 2, slot3, -1)
    less = (key3[None, :] >= 0) & (key3[None, :] < key3[:, None])
    rank3 = jnp.where(key3 >= 0, jnp.sum(less.astype(jnp.int32), axis=1) // 2, -1)
    by_rank = (lax.broadcasted_iota(jnp.int32, (used, 3 * cons), 0) == rank3[None, :]).astype(BF16)
    by_slot = (key3[:, None] == lax.broadcasted_iota(jnp.int32, (3 * cons, coarse_len), 1)).astype(BF16)
    pick_used = dot(by_rank, by_slot).astype(BF16)
    used_cols = lax.dot_general(
        c_rows, pick_used, (((1,), (1,)), ((), ())), preferred_element_type=F32
    ).astype(BF16)
    pick_rows = lax.dynamic_slice_in_dim(pick_used, section * coarse_part, coarse_part, axis=1)
    used_part = (0.25 * dot(pick_rows, used_cols)).astype(BF16)
    used_part = jnp.pad(used_part, ((0, 0), (0, cons - used)))

    matched = jnp.where(want_a, res_a, res_b)
    assembled = (residual + dot(selector, matched)).astype(BF16)
    values_part = lax.dot_general(
        weights, assembled, (((0,), (0,)), ((), ())), preferred_element_type=F32
    ).astype(BF16)

    packed = jnp.concatenate([assembled, values_part, used_part, far_code])
    around = lax.all_gather(packed, "sec", axis=0)
    assembled_all = around[:, :face_len].reshape(-1, around.shape[2])
    values = jnp.sum(around[:, face_len : face_len + cons].astype(F32), axis=0).astype(BF16)
    at = face_len + cons
    used_block = jnp.sum(around[:, at : at + used].astype(F32), axis=0).astype(BF16)
    far_codes = around[:, at + used :]
    correction = dot(n_rows, assembled_all)

    coarse_load = jnp.concatenate([values, used_block])
    out = jnp.concatenate([correction.astype(BF16), coarse_load])
    far2_mine = swap_by_section(coarse_load, KINDS[:2])
    far3_mine = swap_by_section(values, KINDS[2:])
    cor_b = swap_columns(out, "B")
    cor_a = swap_columns(out, "A")
    far_mine = jnp.concatenate([far2_mine, far3_mine])
    far_other = swap_cores(far_mine)

    sign = jnp.where(core == 0, 1, -1)
    c0 = lambda x, y: jnp.where(core == 0, x, y)
    window = parts3 + [
        dec(c0(far_codes[0], far_codes[1]), sign * off2),
        dec(c0(far_codes[1], far_codes[0]), -sign * off2),
        dec(c0(far_codes[2], far_codes[3]), sign * off3),
        dec(c0(far_codes[3], far_codes[2]), -sign * off3),
    ]
    clus = jnp.concatenate([p[0] for p in window])
    slot = jnp.concatenate([p[1] for p in window])
    inside = (clus >= 0) & (clus < 5)
    same_less = (clus[None, :] == clus[:, None]) & (slot[None, :] < slot[:, None])
    rank = jnp.sum(same_less.astype(jnp.int32), axis=1) // 2
    order = [0, off1, -off1, sign * off2, -sign * off2]
    place = sum(jnp.where(clus == 2 + order[m], m, 0) for m in range(1, 5))
    code = jnp.where(inside, place * used + rank, -1)
    unknowns = 5 * used
    spread = (lax.broadcasted_iota(jnp.int32, (unknowns, 7 * cons), 0) == code[None, :]).astype(BF16)
    nbr_code = jnp.where(want_a, code[cons : 2 * cons], code[2 * cons : 3 * cons])
    pair_code = jnp.concatenate([code[:cons], nbr_code])
    gather = (pair_code[:, None] == lax.broadcasted_iota(jnp.int32, (2 * cons, unknowns), 1)).astype(BF16)
    weights_nbr = jnp.where(want_a, near_a[:face_len], near_b[:face_len])
    weights_pair = jnp.concatenate([weights, dot(selector, weights_nbr).astype(BF16)], axis=1)

    far = coarse_load.shape[0]
    values_near = jnp.concatenate(
        [
            values,
            cor_a[face_len : face_len + cons],
            cor_b[face_len : face_len + cons],
            far_mine[:cons],
            far_other[:cons],
            far_mine[far:],
            far_other[far:],
        ]
    )
    blocks = jnp.stack(
        [
            used_block,
            cor_a[face_len + cons :],
            cor_b[face_len + cons :],
            far_mine[cons:far],
            far_other[cons:far],
        ]
    )[:, :, :used]
    rhs = dot(spread, values_near).astype(BF16).reshape(5, used, -1)
    coarse = jnp.einsum("quv,qvc->quc", blocks, rhs, preferred_element_type=F32).astype(BF16)
    picked = dot(gather, coarse.reshape(unknowns, -1)).astype(BF16)
    facing = dot(selector, jnp.where(want_a, cor_a[:face_len], cor_b[:face_len]))
    precond = (0.5 * (correction + facing + dot(weights_pair, picked))).astype(BF16)

    precond_all = lax.all_gather(precond, "sec", axis=0, tiled=True)
    image = dot(s_rows, precond_all).astype(BF16)
    return precond[None], image[None]


def solution(mesh):
    placed = (
        P("sub", "sec", None),
        P("sub", "sec", None),
        P("sub", "sec", None),
        P("sub", "sec", None),
        P("sub", "sec", None),
        P("sub", "sec", None),
        P("sub", None),
        P("sub", "sec"),
        P("sub", None),
    )
    return jax.shard_map(
        local,
        mesh=mesh,
        in_specs=placed,
        out_specs=(P("sub", "sec", None), P("sub", "sec", None)),
        check_vma=False,
    )
```

```python
import jax
import jax.numpy as jnp
from jax import lax
from jax.experimental import pallas as pl
from jax.experimental.pallas import tpu as pltpu
from jax.sharding import PartitionSpec as P


F32 = jnp.float32
BF16 = jnp.bfloat16
KINDS = ("A2", "B2", "A3", "B3")


def partner(kind, i, count):
    forward = {
        "A": i % 2 == 0,
        "B": i % 2 == 1,
        "A2": i % 4 < 2,
        "B2": i % 4 >= 2,
        "A3": i % 2 == 0,
        "B3": i % 2 == 1,
    }[kind]
    step = {"2": 2, "3": 3}.get(kind[-1], 1)
    return (i + step if forward else i - step) % count


def swap_columns(array, kind):
    count = lax.axis_size("sub")
    return lax.ppermute(array, "sub", [(i, partner(kind, i, count)) for i in range(count)])


def swap_by_section(array, kinds):
    sections, count = lax.axis_size("sec"), lax.axis_size("sub")
    moves = [
        (s * count + i, s * count + partner(kinds[s % len(kinds)], i, count))
        for s in range(sections)
        for i in range(count)
    ]
    return lax.ppermute(array, ("sec", "sub"), moves)


def swap_cores(array):
    return lax.ppermute(array, "sec", [(i, i ^ 1) for i in range(lax.axis_size("sec"))])


def swap_chips(array):
    return lax.ppermute(array, "sec", [(i, i ^ 2) for i in range(lax.axis_size("sec"))])


def fetch_kernel(*refs):
    arrays = (len(refs) - 2) // 2
    sems = refs[-1]
    copies = [
        pltpu.make_async_copy(refs[k], refs[arrays + k], sems.at[k]) for k in range(arrays)
    ]
    for copy in copies:
        copy.start()
    for copy in copies:
        copy.wait()
    glued = refs[2 * arrays]
    table = refs[arrays][...]
    section = lax.axis_index("sec")
    place = lax.broadcasted_iota(jnp.int32, table.shape, 1)
    for row, face in enumerate((section, section ^ 2)):
        glued[row : row + 1, :] = jnp.zeros((1, glued.shape[1]), jnp.int32) + jnp.sum(
            jnp.where(place == face, table, 0), axis=1, keepdims=True
        )


def fetch(*arrays):
    return pl.pallas_call(
        fetch_kernel,
        out_shape=[pltpu.VMEM(a.shape, a.dtype) for a in arrays] + [pltpu.VMEM((2, 128), jnp.int32)],
        in_specs=[pl.BlockSpec(memory_space=pl.ANY)] * len(arrays),
        out_specs=[pl.BlockSpec(memory_space=pltpu.VMEM)] * (len(arrays) + 1),
        scratch_shapes=[pltpu.SemaphoreType.DMA((len(arrays),))],
        name="fetch",
    )(*arrays)


def one_hot(index, length):
    return (index[:, None] == lax.broadcasted_iota(jnp.int32, (index.shape[0], length), 1)).astype(BF16)


def dot(a, b):
    return jnp.dot(a, b, preferred_element_type=F32)


def encode_dof(dof, column, count, coarse_len):
    near = (dof // coarse_len - column + 1) % count
    slot = dof % coarse_len
    parts = -(-coarse_len // 128)
    rows = jnp.stack([near * parts + slot // 128, slot % 128]).astype(BF16)
    return jnp.pad(rows, ((0, 14), (0, 0)))


def decode_dof(rows, offset, coarse_len):
    parts = -(-coarse_len // 128)
    whole = rows[:2].astype(F32).astype(jnp.int32)
    cluster = offset + 1 + whole[0] // parts
    return cluster, whole[0] % parts * 128 + whole[1]


def local(
    schur,
    neumann,
    constraint_weights,
    coarse_inverse,
    solution,
    load,
    neighbours,
    face_index,
    coarse_dof,
):
    s_rows, n_rows, weights = schur[0], neumann[0], constraint_weights[0]
    c_rows = coarse_inverse[0]
    face_len, cons = weights.shape
    coarse_part, coarse_len = c_rows.shape
    used = cons // 2
    column, section = lax.axis_index("sub"), lax.axis_index("sec")
    count = lax.axis_size("sub")
    core = section % 2

    even = column % 2 == 0
    off1 = jnp.where(even, 1, -1)
    off2 = jnp.where(column % 4 < 2, 2, -2)
    off3 = jnp.where(even, 3, -3)
    dec = lambda rows, off: decode_dof(rows, off, coarse_len)

    def by_chip(own, peer):
        low = section // 2 == 0
        return jnp.concatenate([jnp.where(low, own, peer), jnp.where(low, peer, own)])

    def by_core(mine, other):
        even_core = jnp.where(core == 0, mine, other)
        odd_core = jnp.where(core == 0, other, mine)
        pieces = [even_core[:face_len], odd_core[:face_len], even_core[face_len:], odd_core[face_len:]]
        return jnp.concatenate(pieces)

    iterate_peer = swap_chips(solution[0])
    n_peer = swap_chips(n_rows)
    _, weights, own_dof, face_index, load_rows, iterate_own, n_own, glued = fetch(
        neighbours, weights, coarse_dof, face_index, load[0], solution[0], n_rows
    )
    own_code = encode_dof(own_dof[0], column, count, coarse_len)
    first = jnp.concatenate([weights, own_code])
    near_b = swap_columns(first, "B")
    near_a = swap_columns(first, "A")
    iterate_other = swap_cores(solution[0])
    iterate_both = swap_cores(iterate_peer)
    iterate = by_core(by_chip(iterate_own, iterate_peer), by_chip(iterate_other, iterate_both))
    residual = load_rows.astype(F32) - dot(s_rows, iterate)

    residual_half = residual.astype(BF16)
    res_b = swap_columns(residual_half, "B")
    res_a = swap_columns(residual_half, "A")
    far_code = swap_by_section(own_code, KINDS)

    from_a = ((glued - column - off1) % count) == 0

    def wants_a(part, rows, width):
        return jnp.broadcast_to(from_a[part : part + 1, :width], (rows, width))

    selector = one_hot(face_index[0], face_len)

    own_place = dec(own_code, 0)
    parts3 = [own_place, dec(near_a[face_len:], off1), dec(near_b[face_len:], -off1)]
    clus3 = jnp.concatenate([p[0] for p in parts3])
    slot3 = jnp.concatenate([p[1] for p in parts3])
    key3 = jnp.where(clus3 == 2, slot3, -1)
    less = (key3[None, :] >= 0) & (key3[None, :] < key3[:, None])
    rank3 = jnp.where(key3 >= 0, jnp.sum(less.astype(jnp.int32), axis=1) // 2, -1)
    by_rank = (lax.broadcasted_iota(jnp.int32, (used, 3 * cons), 0) == rank3[None, :]).astype(BF16)
    by_slot = one_hot(key3, coarse_len)
    pick_used = dot(by_rank, by_slot).astype(BF16)
    used_cols = lax.dot_general(c_rows, pick_used, (((1,), (1,)), ((), ())), preferred_element_type=F32).astype(BF16)
    pick_rows = lax.dynamic_slice_in_dim(pick_used, section * coarse_part, coarse_part, axis=1)
    used_part = (0.25 * dot(pick_rows, used_cols)).astype(BF16)
    used_part = jnp.pad(used_part, ((0, 0), (0, cons - used)))

    weights_nbr = jnp.where(wants_a(0, face_len, cons), near_a[:face_len], near_b[:face_len])
    face_rows = jnp.pad(face_index.reshape(-1, cons).astype(BF16), ((0, 16 - face_len // cons), (0, 0)))
    weights_two = jnp.concatenate([weights, dot(selector, weights_nbr).astype(BF16), face_rows])
    weights_two_peer = swap_chips(weights_two)

    matched = jnp.where(wants_a(0, face_len, 128), res_a, res_b)
    assembled = (residual + dot(selector, matched)).astype(BF16)
    values_part = lax.dot_general(
        weights, assembled, (((0,), (0,)), ((), ())), preferred_element_type=F32
    ).astype(BF16)

    packed = jnp.concatenate([assembled, values_part, used_part, far_code])
    around = lax.all_gather(packed, "sec", axis=0)
    assembled_all = around[:, :face_len].reshape(-1, around.shape[2])
    values = jnp.sum(around[:, face_len : face_len + cons].astype(F32), axis=0).astype(BF16)
    at = face_len + cons
    used_block = jnp.sum(around[:, at : at + used].astype(F32), axis=0).astype(BF16)
    far_codes = around[:, at + used :]

    coarse_load = jnp.concatenate([values, used_block])
    far3_mine = swap_by_section(values, KINDS[2:])
    far2_mine = swap_by_section(coarse_load, KINDS[:2])
    correction = jnp.concatenate([dot(n_own, assembled_all), dot(n_peer, assembled_all)])
    out = jnp.concatenate([correction.astype(BF16), coarse_load])
    cor_b = swap_columns(out, "B")
    cor_a = swap_columns(out, "A")
    far_mine = jnp.concatenate([far2_mine, far3_mine])
    far_other = swap_cores(far_mine)

    sign = jnp.where(core == 0, 1, -1)
    c0 = lambda x, y: jnp.where(core == 0, x, y)
    window = parts3 + [
        dec(c0(far_codes[0], far_codes[1]), sign * off2),
        dec(c0(far_codes[1], far_codes[0]), -sign * off2),
        dec(c0(far_codes[2], far_codes[3]), sign * off3),
        dec(c0(far_codes[3], far_codes[2]), -sign * off3),
    ]
    clus = jnp.concatenate([p[0] for p in window])
    slot = jnp.concatenate([p[1] for p in window])
    inside = (clus >= 0) & (clus < 5)
    same_less = (clus[None, :] == clus[:, None]) & (slot[None, :] < slot[:, None])
    rank = jnp.sum(same_less.astype(jnp.int32), axis=1) // 2
    order = [0, off1, -off1, sign * off2, -sign * off2]
    place = sum(jnp.where(clus == 2 + order[m], m, 0) for m in range(1, 5))
    code = jnp.where(inside, place * used + rank, -1)
    unknowns = 5 * used
    spread = (lax.broadcasted_iota(jnp.int32, (unknowns, 7 * cons), 0) == code[None, :]).astype(BF16)

    two = 2 * face_len
    far = coarse_load.shape[0]
    values_near = jnp.concatenate(
        [
            values,
            cor_a[two : two + cons],
            cor_b[two : two + cons],
            far_mine[:cons],
            far_other[:cons],
            far_mine[far:],
            far_other[far:],
        ]
    )
    blocks = jnp.stack(
        [
            used_block,
            cor_a[two + cons :],
            cor_b[two + cons :],
            far_mine[cons:far],
            far_other[cons:far],
        ]
    )[:, :, :used]
    rhs = dot(spread, values_near).astype(BF16).reshape(5, used, -1)
    coarse = jnp.einsum("quv,qvc->quc", blocks, rhs, preferred_element_type=F32).astype(BF16)
    coarse = coarse.reshape(unknowns, -1)

    def finish(part, select, rows):
        first_row = part * face_len
        near = jnp.where(
            wants_a(part, face_len, 128), cor_a[first_row : first_row + face_len], cor_b[first_row : first_row + face_len]
        )
        nbr_code = jnp.where(from_a[part, :cons], code[cons : 2 * cons], code[2 * cons : 3 * cons])
        pick = one_hot(jnp.concatenate([code[:cons], nbr_code]), unknowns)
        both = jnp.concatenate([rows[:face_len], rows[face_len:two]], axis=1)
        added = dot(both, dot(pick, coarse).astype(BF16))
        return (0.5 * (correction[first_row : first_row + face_len] + dot(select, near) + added)).astype(BF16)

    face_peer = weights_two_peer[two : two + face_len // cons].astype(F32).astype(jnp.int32).reshape(-1)
    precond = finish(0, selector, weights_two)
    precond_peer = finish(1, one_hot(face_peer, face_len), weights_two_peer)

    precond_two = by_chip(precond, precond_peer)
    precond_other = swap_cores(precond_two)
    image = dot(s_rows, by_core(precond_two, precond_other)).astype(BF16)
    return precond[None], image[None]


def solution(mesh):
    placed = (
        P("sub", "sec", None),
        P("sub", "sec", None),
        P("sub", "sec", None),
        P("sub", "sec", None),
        P("sub", "sec", None),
        P("sub", "sec", None),
        P("sub", None),
        P("sub", "sec"),
        P("sub", None),
    )
    return jax.shard_map(
        local,
        mesh=mesh,
        in_specs=placed,
        out_specs=(P("sub", "sec", None), P("sub", "sec", None)),
        check_vma=False,
    )
```
